32 devices in a mesh: grp: 4 (over y, x), tp: 8 (over z, core).
Axes of the slice: x: 2, y: 2, z: 4, core: 2. Of those that a mesh axis runs over, the one named last changes fastest.
Arguments:
- teacher_in: bfloat16 [192, 8192], P('tp', 'grp'), may hold values from -6 to 6
- teacher_gate: bfloat16 [8192, 28672], P('grp', 'tp'), may hold values from -0.0625 to 0.0625
- teacher_up: bfloat16 [8192, 28672], P('grp', 'tp'), may hold values from -0.0625 to 0.0625
- teacher_down: bfloat16 [28672, 8192], P('tp', 'grp'), may hold values from -0.046875 to 0.046875
- student_in: bfloat16 [192, 4096], P('tp', 'grp'), may hold values from -6 to 6
- student_gate: bfloat16 [4096, 14336], P('grp', 'tp'), may hold values from -0.09375 to 0.09375
- student_up: bfloat16 [4096, 14336], P('grp', 'tp'), may hold values from -0.09375 to 0.09375
- student_down: bfloat16 [14336, 4096], P('tp', 'grp'), may hold values from -0.046875 to 0.046875
- projector: bfloat16 [4096, 4, 2048], P('grp', None, 'tp'), may hold values from -0.09375 to 0.09375
Outputs:
- grad_input: float32 [192, 4096], P('tp', 'grp')
- grad_gate: float32 [4096, 14336], P('grp', 'tp')
- grad_up: float32 [4096, 14336], P('grp', 'tp')
- grad_down: float32 [14336, 4096], P('tp', 'grp')
- grad_projector: float32 [4096, 4, 2048], P('grp', None, 'tp')
The draws below stay inside these ranges and needn't reach their ends.
All inputs are finite; a program needn't handle non-finite values.
Results may differ from the reference program's by a relative error of at most 0.017.
Values may be sent and summed in bfloat16 or wider, within the bound.
No kernel may reach another device: no remote copies, remote signals or barrier semaphores. Data moves between devices by JAX's collectives and lax.ppermute only.
A program may use at most 192 MiB of HBM per device.

```python
import jax
import jax.numpy as jnp

DT = 8192
FT = 28672
DS = 4096
FS = 14336
TOKENS = 192
N_GRP = 4


def strengthened(result, own_key, source, target, parts, factor):
    owner, partner = [(jnp.arange(result.shape[axis_at]) // (result.shape[axis_at] // parts)).reshape([-1 if axis == axis_at else 1 for axis in range(result.ndim)]) for axis_at in (source, target)]
    chosen = jax.random.permutation(own_key, parts)[partner]
    strong = (owner == chosen) | (owner == (partner + parts // 2) % parts)
    return jnp.where(strong, factor * result, result)


def shard_levels(stream_key, dims, pieces, least, high):
    level = 1.0
    for position, parts in pieces:
        heights = jax.random.uniform(jax.random.fold_in(jax.random.fold_in(stream_key, 6), position), (parts,), jnp.float32, least / len(pieces), high / len(pieces))
        level = level * jnp.repeat(jnp.exp(heights), dims[position] // parts).reshape((-1,) + (1,) * (len(dims) - 1 - position))
    return level


def gaussian(stream_key, dims, scale, reach, split=(), dtype=jnp.bfloat16):
    result = scale * jax.random.normal(stream_key, dims, jnp.float32)
    if split:
        result = result * shard_levels(stream_key, dims, split, -0.22, 0.18)
    return jnp.clip(result, -reach, reach).astype(dtype)


def bell_draw_with(own_key, extent, deviation, reach, cuts, heavy, held_as=jnp.bfloat16):
    values = deviation * jax.random.normal(own_key, extent, jnp.float32)
    if cuts:
        values = values * shard_levels(own_key, extent, cuts, -0.22, 0.18)
    return jnp.clip(strengthened(values, jax.random.fold_in(own_key, 3), *heavy), -reach, reach).astype(held_as)


def setup_inputs(seed: int = 0) -> dict:
    arg_keys = jax.random.split(jax.random.key(seed), 10)
    teacher_in = gaussian(arg_keys[0], (TOKENS, DT), 1.0, 6.0, ((0, 8), (1, 4)))
    teacher_gate = gaussian(arg_keys[1], (DT, FT), DT ** -0.5, 0.0625, ((0, 4), (1, 8)))
    teacher_up = gaussian(arg_keys[2], (DT, FT), DT ** -0.5, 0.0625, ((0, 4), (1, 8)))
    teacher_down = bell_draw_with(arg_keys[3], (FT, DT), FT ** -0.5, 0.046875, ((0, 8), (1, 4)), (0, 1, 8, 2.0))
    student_in = gaussian(arg_keys[4], (TOKENS, DS), 1.0, 6.0, ((0, 8), (1, 4)))
    student_gate = gaussian(arg_keys[5], (DS, FS), DS ** -0.5, 0.09375, ((0, 4), (1, 8)))
    student_up = gaussian(arg_keys[6], (DS, FS), DS ** -0.5, 0.09375, ((0, 4), (1, 8)))
    student_down = gaussian(arg_keys[7], (FS, DS), FS ** -0.5, 0.046875, ((0, 8), (1, 4)))
    projector = gaussian(arg_keys[8], (DS, N_GRP, DT // N_GRP), DS ** -0.5, 0.09375, ((0, 4), (2, 8)))
    return dict(teacher_in=teacher_in, teacher_gate=teacher_gate, teacher_up=teacher_up, teacher_down=teacher_down, student_in=student_in, student_gate=student_gate, student_up=student_up, student_down=student_down, projector=projector)


def reference(teacher_in, teacher_gate, teacher_up, teacher_down, student_in, student_gate, student_up, student_down, projector):
    bf = jnp.bfloat16
    fl = jnp.float32
    teacher_pre = jnp.dot(teacher_in, teacher_gate, preferred_element_type=fl)
    teacher_lin = jnp.dot(teacher_in, teacher_up, preferred_element_type=fl)
    teacher_hidden = (jax.nn.silu(teacher_pre) * teacher_lin).astype(bf)
    teacher_feature = jnp.dot(teacher_hidden, teacher_down, preferred_element_type=fl).astype(bf)
    gate_values = jnp.dot(student_in, student_gate, preferred_element_type=fl)
    up_values = jnp.dot(student_in, student_up, preferred_element_type=fl)
    student_hidden = (jax.nn.silu(gate_values) * up_values).astype(bf)
    student_feature = jnp.dot(student_hidden, student_down, preferred_element_type=fl).astype(bf)
    proj_matrix = projector.reshape(projector.shape[0], -1)
    projected = jnp.dot(student_feature, proj_matrix, preferred_element_type=fl)
    residual_grad = (projected - teacher_feature.astype(fl)).astype(bf)
    grad_projector = jnp.dot(student_feature.T, residual_grad, preferred_element_type=fl).reshape(projector.shape)
    feature_grad = jnp.dot(residual_grad, proj_matrix.T, preferred_element_type=fl).astype(bf)
    grad_down = jnp.dot(student_hidden.T, feature_grad, preferred_element_type=fl)
    hidden_grad = jnp.dot(feature_grad, student_down.T, preferred_element_type=fl)
    sigmoid_gate = jax.nn.sigmoid(gate_values)
    gate_grad = (hidden_grad * up_values * sigmoid_gate * (1.0 + gate_values * (1.0 - sigmoid_gate))).astype(bf)
    up_grad = (hidden_grad * gate_values * sigmoid_gate).astype(bf)
    grad_gate = jnp.dot(student_in.T, gate_grad, preferred_element_type=fl)
    grad_up = jnp.dot(student_in.T, up_grad, preferred_element_type=fl)
    grad_input = jnp.dot(gate_grad, student_gate.T, preferred_element_type=fl) + jnp.dot(up_grad, student_up.T, preferred_element_type=fl)
    return grad_input, grad_gate, grad_up, grad_down, grad_projector
```

```python
import jax
import jax.numpy as jnp
from jax import lax
from jax.sharding import PartitionSpec as P

BF = jnp.bfloat16
FL = jnp.float32


def swap(x, axis, size, k):
    return lax.ppermute(x, axis, [(i, i ^ k) for i in range(size)])


def dot(a, b):
    return jnp.dot(a, b, preferred_element_type=FL)


def dot_t(a, b):
    return lax.dot_general(a, b, (((1,), (1,)), ((), ())), preferred_element_type=FL)


def t_dot(a, b):
    return lax.dot_general(a, b, (((0,), (0,)), ((), ())), preferred_element_type=FL)


def make_body(n_grp, n_tp):
    def grp(x, k):
        return swap(x, "grp", n_grp, k)

    def tp(x, k):
        return swap(x, "tp", n_tp, k)

    def tp_pieces(x):
        even = {0: x}
        for k in range(2, n_tp, 2):
            even[k] = tp(x, k)
        out = []
        for k in range(0, n_tp, 2):
            out += [even[k], tp(even[k], 1)]
        return out

    def grp_scatter(parts):
        total = parts[0].astype(FL)
        for k in range(1, n_grp):
            total = total + grp(parts[k].astype(BF), k).astype(FL)
        return total

    def grp_gather(own):
        return [own] + [grp(own, k) for k in range(1, n_grp)]

    def tp_sum(y, core):
        half = y.shape[1] // 2
        y = y.astype(BF)
        left, right = y[:, :half], y[:, half:]
        mine = jnp.where(core == 0, left, right)
        other = jnp.where(core == 0, right, left)
        total = mine.astype(FL) + tp(other, 1).astype(FL)
        k = 2
        while k < n_tp:
            total = total.astype(BF)
            total = total.astype(FL) + tp(total, k).astype(FL)
            k *= 2
        total = total.astype(BF)
        other = tp(total, 1)
        return jnp.where(
            core == 0,
            jnp.concatenate([total, other], axis=1),
            jnp.concatenate([other, total], axis=1),
        )

    def body(
        teacher_in,
        teacher_gate,
        teacher_up,
        teacher_down,
        student_in,
        student_gate,
        student_up,
        student_down,
        projector,
    ):
        g = lax.axis_index("grp")
        t = lax.axis_index("tp")
        core = t % 2
        share = student_in.shape[0]
        tokens = share * n_tp
        rows = tokens // n_grp

        order = lax.broadcasted_iota(jnp.int32, (tokens, tokens), 0)
        token = ((order // rows) ^ g) * rows + order % rows
        source = ((token // share) ^ t) * share + token % share
        pick = (source == lax.broadcasted_iota(jnp.int32, (tokens, tokens), 1)).astype(BF)

        def local_rows(x):
            return dot(pick, jnp.concatenate(tp_pieces(x), axis=0)).astype(BF)

        def chunks(y):
            return [y[k * rows : (k + 1) * rows] for k in range(n_grp)]

        student_rows = local_rows(student_in)
        teacher_rows = local_rows(teacher_in)

        gate_values = grp_scatter(chunks(dot(student_rows, student_gate).astype(BF)))
        up_values = grp_scatter(chunks(dot(student_rows, student_up).astype(BF)))
        sigmoid_gate = jax.nn.sigmoid(gate_values)
        student_hidden = (gate_values * sigmoid_gate * up_values).astype(BF)
        hidden_rows = jnp.concatenate(grp_gather(student_hidden), axis=0)
        student_feature = tp_sum(dot(hidden_rows, student_down), core)

        width = teacher_gate.shape[1]
        pieces = 2
        step = width // pieces
        teacher_sums = 0.0
        for p in range(pieces):
            cut = slice(p * step, (p + 1) * step)
            pre = grp_scatter(chunks(dot(teacher_rows, teacher_gate[:, cut]).astype(BF)))
            lin = grp_scatter(chunks(dot(teacher_rows, teacher_up[:, cut]).astype(BF)))
            teacher_hidden = (jax.nn.silu(pre) * lin).astype(BF)
            teacher_hidden = jnp.concatenate(grp_gather(teacher_hidden), axis=0)
            teacher_sums = teacher_sums + dot(teacher_hidden, teacher_down[cut])
        teacher_sums = teacher_sums.astype(BF)
        cols = teacher_sums.shape[1] // n_tp

        def teacher_cols(k):
            return lax.dynamic_slice_in_dim(teacher_sums, (t ^ k) * cols, cols, axis=1)

        teacher_share = 0.0
        for k in range(0, n_tp, 2):
            both = teacher_cols(k).astype(FL) + tp(teacher_cols(k + 1), 1).astype(FL)
            if k:
                both = tp(both.astype(BF), k).astype(FL)
            teacher_share = teacher_share + both
        teacher_share = teacher_share.astype(BF).astype(FL)

        proj_blocks = [
            lax.dynamic_index_in_dim(projector, g ^ k, axis=1, keepdims=False)
            for k in range(n_grp)
        ]
        proj_local = jnp.concatenate(proj_blocks, axis=1)
        block = projector.shape[2]

        def from_peer(x, k):
            return jnp.concatenate([x[(k ^ m) * rows : ((k ^ m) + 1) * rows] for m in range(n_grp)])

        projected = dot(student_feature, proj_local)
        residual = projected[:, :block] - teacher_share
        for k in range(1, n_grp):
            got = grp(projected[:, k * block : (k + 1) * block].astype(BF), k)
            residual = residual + from_peer(got, k).astype(FL)
        residual = residual.astype(BF)
        got = grp_gather(residual)
        residual_rows = jnp.concatenate(
            [from_peer(got[k], k) if k else got[k] for k in range(n_grp)], axis=1
        )
        feature_grad = tp_sum(dot_t(residual_rows, proj_local), core)

        ordered = [
            lax.dynamic_index_in_dim(
                residual_rows.reshape(tokens, n_grp, block), g ^ k, axis=1, keepdims=False
            )
            for k in range(n_grp)
        ]
        grad_projector = t_dot(student_feature, jnp.concatenate(ordered, axis=1)).reshape(
            projector.shape
        )
        grad_down = t_dot(hidden_rows, feature_grad)

        gate_factor = (
            up_values * sigmoid_gate * (1.0 + gate_values * (1.0 - sigmoid_gate))
        ).astype(BF)
        up_factor = (gate_values * sigmoid_gate).astype(BF)
        gate_factor = grp_gather(gate_factor)
        up_factor = grp_gather(up_factor)

        hidden_grad = grp_scatter(chunks(dot_t(feature_grad, student_down).astype(BF))).astype(BF)
        hidden_grad = grp_gather(hidden_grad)
        gate_grad = jnp.concatenate(
            [(h.astype(FL) * f.astype(FL)).astype(BF) for h, f in zip(hidden_grad, gate_factor)]
        )
        up_grad = jnp.concatenate(
            [(h.astype(FL) * f.astype(FL)).astype(BF) for h, f in zip(hidden_grad, up_factor)]
        )
        input_sums = (dot_t(gate_grad, student_gate) + dot_t(up_grad, student_up)).astype(BF)
        pitch = -(-share // 16) * 16
        slot = lax.broadcasted_iota(jnp.int32, (pitch * n_tp, tokens), 0)
        wanted = ((slot // pitch) ^ t) * share + slot % pitch
        place = ((wanted // rows) ^ g) * rows + wanted % rows
        column = lax.broadcasted_iota(jnp.int32, (pitch * n_tp, tokens), 1)
        send = dot(((place == column) & (slot % pitch < share)).astype(BF), input_sums).astype(BF)

        def piece(k):
            return send[k * pitch : k * pitch + share]

        grad_input = 0.0
        for k in range(0, n_tp, 2):
            both = piece(k).astype(FL) + tp(piece(k + 1), 1).astype(FL)
            if k:
                both = tp(both.astype(BF), k).astype(FL)
            grad_input = grad_input + both

        grad_gate = t_dot(student_rows, gate_grad)
        grad_up = t_dot(student_rows, up_grad)
        return grad_input, grad_gate, grad_up, grad_down, grad_projector

    return body


def solution(mesh):
    placed = (
        P("tp", "grp"),
        P("grp", "tp"),
        P("grp", "tp"),
        P("tp", "grp"),
        P("tp", "grp"),
        P("grp", "tp"),
        P("grp", "tp"),
        P("tp", "grp"),
        P("grp", None, "tp"),
    )
    return jax.shard_map(
        make_body(mesh.shape["grp"], mesh.shape["tp"]),
        mesh=mesh,
        in_specs=placed,
        out_specs=(
            P("tp", "grp"),
            P("grp", "tp"),
            P("grp", "tp"),
            P("tp", "grp"),
            P("grp", None, "tp"),
        ),
        check_vma=False,
    )
```
